512 devices in a mesh: row: 16 (over x_lo, z), col: 32 (over y, x_hi, core).
Axes of the slice: x: 4 (x_hi: 2, x_lo: 2; x = x_hi * 2 + x_lo), y: 8, z: 8, core: 2. Of those that a mesh axis runs over, the one named last changes fastest.
Arguments:
- protocols: float32 [20, 65536], P(None, ('row', 'col')), may hold values from -6 to 6
- w_in: float32 [20, 256], replicated, may hold values from -1.25 to 1.25
- b_in: float32 [256], replicated, may hold values from -3 to 3
- w_out: float32 [256, 64], replicated, may hold values from -0.21875 to 0.21875
- solved: float32 [32, 65536], P(None, ('row', 'col')), may hold values from -0.5 to 0.5
- probes: float32 [32, 65536], P(None, ('row', 'col')), may hold values from -6 to 6
- window_blocks: int32 [16], replicated, may hold values from 0 to 31
Outputs:
- col_grad: float32 [64, 65536], P(None, ('row', 'col'))
- grad_in: float32 [20, 256], replicated
- grad_bias: float32 [256], replicated
- grad_out: float32 [256, 64], replicated
The draws below stay inside these ranges and needn't reach their ends.
Inputs may be any that keep to these rules, and one draw needn't show every extreme that they name: Window block r is the 128 protocols held at index r of row and index window_blocks[r] of col.
All inputs are finite; a program needn't handle non-finite values.
Results may differ from the reference program's by a relative error of at most 0.0003.
Values sent between devices are 32-bit elements; how exact they have to be, the bound alone decides.
A program may use at most 64 MiB of HBM per device.

```python
import jax
import jax.numpy as jnp
from jax import lax

P_SIZE = 20
H = 256
F = 64
Q = 32
CD = 128
GROUPS = 16
WIN = 2048
N = 65536
N_ROW = 16
N_COL = 32


def place_ends(result, key, least, high):
    longest = result.shape.index(max(result.shape))
    spots = []
    for shift in (0, 1):
        where = [jax.random.randint(jax.random.fold_in(key, axis), (), 0, length) for axis, length in enumerate(result.shape)]
        where[longest] = (where[longest] + shift) % result.shape[longest]
        spots.append(tuple(where))
    return result.at[spots[0]].set(least).at[spots[1]].set(high)


def levels(key, shape, shards, low, high):
    def one(position, parts):
        steps = jax.random.uniform(jax.random.fold_in(jax.random.fold_in(key, 6), position), (parts,), jnp.float32, low / len(shards), high / len(shards))
        return jnp.repeat(jnp.exp(steps), shape[position] // parts).reshape((-1,) + (1,) * (len(shape) - position - 1))

    factor_of = one(*shards[0])
    for cut in shards[1:]:
        factor_of = factor_of * one(*cut)
    return factor_of


def centred(key, extent, deviation, bound, shards=(), kind=jnp.bfloat16):
    drawn = jax.random.normal(key, extent, jnp.float32) * deviation
    if len(shards) > 0:
        drawn = levels(key, extent, shards, -0.22, 0.18) * drawn
    return jnp.clip(drawn, min=-bound, max=bound).astype(kind)


def setup_inputs(seed: int = 0) -> dict:
    seeds = jax.random.split(jax.random.key(seed), 8)
    protocols = centred(seeds[0], (P_SIZE, N), 1.0, 6.0, ((1, 512),), jnp.float32)
    w_in = centred(seeds[1], (P_SIZE, H), P_SIZE ** -0.5, 1.25, (), jnp.float32)
    b_in = centred(seeds[2], (H,), 0.5, 3.0, (), jnp.float32)
    w_out = centred(seeds[3], (H, F), (H * 25 // 9) ** -0.5, 0.21875, (), jnp.float32)
    solved = centred(seeds[4], (Q, N), 0.08, 0.5, ((1, 512),), jnp.float32)
    probes = centred(seeds[5], (Q, N), 1.0, 6.0, ((1, 512),), jnp.float32)
    window_blocks = place_ends(jax.random.randint(seeds[6], (GROUPS,), 0, N_COL), jax.random.fold_in(seeds[6], 1), 0, N_COL - 1).astype(jnp.int32)
    return dict(protocols=protocols, w_in=w_in, b_in=b_in, w_out=w_out, solved=solved, probes=probes, window_blocks=window_blocks)


HIGHEST = lax.Precision.HIGHEST


def tile_pass(first_feat, first_vec, second_feat, second_vec):
    first_norm = jnp.sum(first_feat * first_feat, 0)
    second_norm = jnp.sum(second_feat * second_feat, 0)
    cross = jnp.einsum("fi,fj->ij", first_feat, second_feat, precision=HIGHEST)
    kern = jnp.exp(-0.5 * (first_norm[:, None] + second_norm[None, :] - 2.0 * cross))
    weigh = jnp.einsum("qi,qj->ij", first_vec, second_vec, precision=HIGHEST) * kern
    first_grad = jnp.einsum("fj,ij->fi", second_feat, weigh, precision=HIGHEST) - first_feat * jnp.sum(weigh, 1)[None, :]
    second_grad = jnp.einsum("fi,ij->fj", first_feat, weigh, precision=HIGHEST) - second_feat * jnp.sum(weigh, 0)[None, :]
    return first_grad, second_grad


def hidden_of(w_in, b_in, inputs):
    return jnp.tanh(jnp.einsum("ph,pn->hn", w_in, inputs, precision=HIGHEST) + b_in[:, None])


def backprop(w_in, w_out, inputs, hidden, grads):
    grad_out = jnp.einsum("hn,fn->hf", hidden, grads, precision=HIGHEST)
    grad_hidden = jnp.einsum("hf,fn->hn", w_out, grads, precision=HIGHEST)
    grad_pre = grad_hidden * (1.0 - hidden * hidden)
    grad_in = jnp.einsum("pn,hn->ph", inputs, grad_pre, precision=HIGHEST)
    return grad_in, jnp.sum(grad_pre, 1), grad_out


def reference(protocols, w_in, b_in, w_out, solved, probes, window_blocks):
    hidden = hidden_of(w_in, b_in, protocols)
    features = jnp.einsum("hf,hn->fn", w_out, hidden, precision=HIGHEST)
    starts = (jnp.arange(N_ROW, dtype=jnp.int32) * N_COL + window_blocks.astype(jnp.int32)) * CD
    window_cols = (starts[:, None] + jnp.arange(CD, dtype=jnp.int32)[None, :]).reshape(-1).astype(jnp.int32)
    win_feat = features[:, window_cols]
    win_vec = solved[:, window_cols]
    count = N // CD
    feat_blocks = features.reshape(F, count, CD).transpose(1, 0, 2)
    probe_blocks = probes.reshape(Q, count, CD).transpose(1, 0, 2)

    def advance(running, pair):
        win_part, col_part = tile_pass(win_feat, win_vec, pair[0], pair[1])
        return running + win_part, col_part

    win_grad, col_parts = lax.scan(advance, jnp.zeros((F, WIN), jnp.float32), (feat_blocks, probe_blocks))
    col_grad = col_parts.transpose(1, 0, 2).reshape(F, N)
    total = col_grad.at[:, window_cols].add(win_grad)
    grad_in, grad_bias, grad_out = backprop(w_in, w_out, protocols, hidden, total)
    return col_grad, grad_in, grad_bias, grad_out
```

```python
import functools

import jax
import jax.numpy as jnp
from jax import lax
from jax.experimental import pallas as pl
from jax.experimental.pallas import tpu as pltpu
from jax.sharding import PartitionSpec as P

F32 = jnp.float32
BF16 = jnp.bfloat16
MESH = pl.DeviceIdType.MESH
RING = (4, 3, 5, 2, 6, 1, 7)


def parts2(value):
    high = value.astype(BF16).astype(F32)
    return high, value - high


def parts3(value):
    high = value.astype(BF16).astype(F32)
    rest = value - high
    middle = rest.astype(BF16).astype(F32)
    return high, middle, rest - middle


def rows(*pieces):
    return jnp.concatenate(pieces, axis=0)


def lanes(*pieces):
    return jnp.concatenate(pieces, axis=1)


def low(value):
    return value.astype(BF16)


def nn(left, right):
    return lax.dot_general(left, right, (((1,), (0,)), ((), ())), preferred_element_type=F32)


def nt(left, right):
    return lax.dot_general(left, right, (((1,), (1,)), ((), ())), preferred_element_type=F32)


def first_layer(w_in, bias):
    at = lax.broadcasted_iota(jnp.int32, (24, w_in.shape[1]), 0)
    full = rows(w_in, jnp.zeros((4, w_in.shape[1]), F32))
    full = jnp.where(at == 20, bias, full)
    h, m, l = parts3(full)
    return low(rows(h, m, h, m, h, l).T)


def second_layer(w_out):
    both = rows(*parts2(w_out))
    turned = both.T
    return low(both), low(lanes(turned, turned))


def hidden_of(first, inputs):
    h, m, l = parts3(inputs)
    return jnp.tanh(nn(first, low(rows(h, h, m, m, l, h))))


def features_of(forward, hid_h, hid_l):
    four = nn(forward, hid_h) + nn(forward, hid_l)
    return four[0:64] + four[64:128]


def ones_row(width):
    at = lax.broadcasted_iota(jnp.int32, (16, width), 0)
    return jnp.where(at == 0, 1.0, 0.0)


def stack_of(feat):
    h, l = parts2(feat)
    return low(rows(h, l, ones_row(feat.shape[1])))


def weighted(acc, own):
    return acc[0:64] + acc[64:128] - own * acc[128:129]


def backprop(back, total, hidden, hid_h, hid_l, inputs):
    h, l = parts2(total)
    grad_hidden = nn(back, low(rows(h, h, l, l)))
    grad_pre = grad_hidden * (1.0 - hidden * hidden)
    pre_h, pre_l = parts2(grad_pre)
    p_h, p_l = parts2(inputs)
    left = low(rows(p_h, p_l))
    below = nt(left, low(pre_h)) + nt(left, low(pre_l))
    both = low(rows(h, l))
    above = nt(both, hid_h) + nt(both, hid_l)
    return above[0:64] + above[64:128], below[0:24] + below[24:48]


def window_sides(feat, solved):
    h, m, l = parts3(feat)
    one = rows(h, m).T
    two = rows(h, l).T
    cross_left = low(lanes(one, one, two))
    s_h, s_l = parts2(solved)
    vec_left = low(rows(s_h, s_l, s_h, s_l).T)
    half = 0.5 * jnp.sum(feat * feat, axis=0, keepdims=True)
    half = jnp.broadcast_to(half, (128, feat.shape[1])).T
    return cross_left, vec_left, lanes(half, half)


def cross_right(feat):
    h, m, l = parts3(feat)
    return low(rows(h, h, m, m, l, h))


def vec_right(vec):
    h, l = parts2(vec)
    return low(rows(h, h, l, l))


def pack(block):
    spot = lax.broadcasted_iota(jnp.int32, (16, 128), 1) // 32
    out = []
    for q in range(4):
        piece = jnp.zeros((16, 128), F32)
        for g in range(4):
            slab = block[16 * g : 16 * g + 16]
            turned = slab if g == q else pltpu.roll(slab, (32 * (g - q)) % 128, 1)
            piece = jnp.where(spot == g, turned, piece)
        out.append(piece)
    return out


def unpack(pieces):
    spot = lax.broadcasted_iota(jnp.int32, (16, 128), 1) // 32
    tiles = []
    for t in range(2):
        slabs = []
        for g in range(4):
            slab = jnp.zeros((16, 128), F32)
            for s in range(4):
                piece = pieces[4 * t + s]
                turned = piece if s == g else pltpu.roll(piece, (32 * (s - g)) % 128, 1)
                slab = jnp.where(spot == s, turned, slab)
            slabs.append(slab)
        tiles.append(rows(*slabs))
    return lanes(*tiles)


def kernel(
    protocols, w_in, b_in, w_out, solved, probes, blocks,
    col_out, in_out, bias_out, out_out,
    cols, win_b, bias_b, wout_b, sol, packed, quarter, ybuf, zbuf,
    hid_f, hid_hi, hid_lo, feat_b, stack_b, cross_b, vec_b,
    colp, colr, grads, scattered, zsum, ysum, gathered,
    local_sem, qs, qr, cs, cr, ys, yr, zs, zr, ps, pr, gs, gr, zs2, zr2, ys2, yr2, as_, ar,
):
    row = lax.axis_index("row")
    col = lax.axis_index("col")
    x_lo, z = row // 8, row % 8
    y, x_hi, core = col // 4, (col // 2) % 2, col % 2
    me = x_hi * 4 + x_lo * 2 + core
    mine = x_hi * 2 + core

    def device(a, b, c, d, e):
        return (b * 8 + d, c * 4 + a * 2 + e)

    def flip(value, bit):
        return 1 - value if bit else value

    group = []
    for k in (6, 7, 4, 5, 2, 3, 1):
        a, b, e = flip(x_hi, k & 4), flip(x_lo, k & 2), flip(core, k & 1)
        group.append((a * 4 + b * 2 + e, device(a, b, y, z, e), k))
    along_y = [((y + k) % 8, device(x_hi, x_lo, (y + k) % 8, z, core)) for k in RING]
    along_z = [((z + k) % 8, device(x_hi, x_lo, y, (z + k) % 8, core)) for k in RING]

    barrier = pltpu.get_barrier_semaphore()
    for who in [g[1] for g in group] + [p[1] for p in along_y] + [p[1] for p in along_z]:
        pl.semaphore_signal(barrier, inc=1, device_id=who, device_id_type=MESH)

    loads = [
        pltpu.make_async_copy(protocols, cols.at[me, pl.ds(0, 20)], local_sem.at[0]),
        pltpu.make_async_copy(solved, sol, local_sem.at[1]),
        pltpu.make_async_copy(probes, cols.at[me, pl.ds(24, 32)], local_sem.at[2]),
        pltpu.make_async_copy(w_in, win_b, local_sem.at[3]),
        pltpu.make_async_copy(b_in, bias_b, local_sem.at[4]),
        pltpu.make_async_copy(w_out, wout_b, local_sem.at[5]),
    ]
    for load in loads:
        load.start()
    at = lax.broadcasted_iota(jnp.int32, (4, 128), 0)
    cols[me, 20:24] = jnp.where(at == 0, 1.0, 0.0)
    for load in loads:
        load.wait()

    owner = (blocks[row] == col).astype(jnp.int32).astype(F32)
    block = rows(cols[me, 0:24], sol[...], jnp.zeros((8, 128), F32)) * owner
    for q, piece in enumerate(pack(block)):
        packed[q] = piece

    def send(source, target, ssem, rsem, who):
        copy = pltpu.make_async_remote_copy(
            src_ref=source, dst_ref=target, send_sem=ssem, recv_sem=rsem,
            device_id=who, device_id_type=MESH,
        )
        copy.start()
        return copy

    def arrive(target, ssem, rsem, who):
        pltpu.make_async_remote_copy(
            src_ref=target, dst_ref=target, send_sem=ssem, recv_sem=rsem,
            device_id=who, device_id_type=MESH,
        ).wait_recv()

    pl.semaphore_wait(barrier, 21)
    started = []

    fours = [(g, who, k) for g, who, k in group if not k & 2]
    for i, (g, who, k) in enumerate(fours):
        q = (g // 4) * 2 + g % 2
        started.append(send(packed.at[q], quarter.at[mine], qs.at[i], qr.at[mine], who))
    for i, (g, who, k) in enumerate(group):
        started.append(send(cols.at[me], cols.at[me], cs.at[i], cr.at[me], who))

    first = first_layer(win_b[...], bias_b[...])
    forward, back = second_layer(wout_b[...])

    quarter[mine] = packed[mine]
    for i, (g, who, k) in enumerate(fours):
        q = (g // 4) * 2 + g % 2
        arrive(quarter.at[q], qs.at[i], qr.at[q], who)
    ybuf[y] = quarter[0] + quarter[1] + quarter[2] + quarter[3]
    for i, (s, who) in enumerate(along_y):
        started.append(send(ybuf.at[y], ybuf.at[y], ys.at[i], yr.at[y], who))

    def columns(chunk):
        spread = lanes(cols[2 * chunk], cols[2 * chunk + 1])
        inputs, vec = spread[0:24], spread[24:56]
        hidden = hidden_of(first, inputs)
        h, l = parts2(hidden)
        h, l = low(h), low(l)
        feat = features_of(forward, h, l)
        hid_f[chunk] = hidden
        hid_hi[chunk] = h
        hid_lo[chunk] = l
        feat_b[chunk] = feat
        stack_b[chunk] = stack_of(feat)
        cross_b[chunk] = cross_right(feat)
        vec_b[chunk] = vec_right(vec)

    for i, (g, who, k) in enumerate(group):
        arrive(cols.at[g], cs.at[i], cr.at[g], who)
    columns(0)
    columns(1)

    for i, (s, who) in enumerate(along_y):
        arrive(ybuf.at[s], ys.at[i], yr.at[s], who)
    merged = ybuf[0]
    for s in range(1, 8):
        merged = merged + ybuf[s]
    zbuf[z] = merged
    for i, (s, who) in enumerate(along_z):
        started.append(send(zbuf.at[z], zbuf.at[z], zs.at[i], zr.at[z], who))

    columns(2)
    columns(3)

    for i, (s, who) in enumerate(along_z):
        arrive(zbuf.at[s], zs.at[i], zr.at[s], who)
    window = unpack([zbuf[s] for s in range(8)])
    win_in = window[0:24]
    win_hidden = hidden_of(first, win_in)
    win_h, win_l = parts2(win_hidden)
    win_h, win_l = low(win_h), low(win_l)
    win_feat = features_of(forward, win_h, win_l)
    cross_left, vec_left, half_win = window_sides(win_feat, window[24:56])
    win_stack = stack_of(win_feat)

    win_acc = jnp.zeros((144, 256), F32)
    above = jnp.zeros((64, 256), F32)
    below = jnp.zeros((24, 256), F32)
    for c in range(4):
        feat = feat_b[c]
        half = 0.5 * jnp.sum(feat * feat, axis=0, keepdims=True)
        kern = jnp.exp(nn(cross_left, cross_b[c]) - half_win - half)
        weigh = kern * nn(vec_left, vec_b[c])
        w_h, w_l = parts2(weigh)
        w_h, w_l = low(w_h), low(w_l)
        part = weighted(nn(win_stack, w_h) + nn(win_stack, w_l), feat)
        colp[2 * c] = part[:, 0:128]
        colp[2 * c + 1] = part[:, 128:256]
        win_acc = win_acc + nt(stack_b[c], w_h) + nt(stack_b[c], w_l)
        inputs = lanes(cols[2 * c, 0:24], cols[2 * c + 1, 0:24])
        more = backprop(back, part, hid_f[c], hid_hi[c], hid_lo[c], inputs)
        above = above + more[0]
        below = below + more[1]
    win_part = weighted(win_acc, win_feat)
    more = backprop(back, win_part, win_hidden, win_h, win_l, win_in)
    above = above + more[0]
    below = below + more[1]

    for p in range(8):
        grads[p, 0:8] = above[8 * p : 8 * p + 8, 0:128]
        grads[p, 8:16] = above[8 * p : 8 * p + 8, 128:256]
        if p < 6:
            t, s = p // 2, p % 2
            grads[p, 16:24] = below[8 * t : 8 * t + 8, 128 * s : 128 * s + 128]
        else:
            grads[p, 16:24] = jnp.zeros((8, 128), F32)

    for i, (g, who, k) in enumerate(group):
        started.append(send(grads.at[g], scattered.at[me], gs.at[i], gr.at[me], who))
    for i, (g, who, k) in enumerate(group):
        started.append(send(colp.at[g], colr.at[me], ps.at[i], pr.at[me], who))
    scattered[me] = grads[me]
    for i, (g, who, k) in enumerate(group):
        arrive(scattered.at[g], gs.at[i], gr.at[g], who)
    total = scattered[0]
    for s in range(1, 8):
        total = total + scattered[s]
    zsum[z] = total
    for i, (s, who) in enumerate(along_z):
        started.append(send(zsum.at[z], zsum.at[z], zs2.at[i], zr2.at[z], who))

    colr[me] = colp[me]
    for i, (g, who, k) in enumerate(group):
        arrive(colr.at[g], ps.at[i], pr.at[g], who)
    col_grad = colr[0]
    for s in range(1, 8):
        col_grad = col_grad + colr[s]
    col_out[...] = col_grad

    for i, (s, who) in enumerate(along_z):
        arrive(zsum.at[s], zs2.at[i], zr2.at[s], who)
    total = zsum[0]
    for s in range(1, 8):
        total = total + zsum[s]
    ysum[y] = total
    for i, (s, who) in enumerate(along_y):
        started.append(send(ysum.at[y], ysum.at[y], ys2.at[i], yr2.at[y], who))
    for i, (s, who) in enumerate(along_y):
        arrive(ysum.at[s], ys2.at[i], yr2.at[s], who)
    total = ysum[0]
    for s in range(1, 8):
        total = total + ysum[s]
    gathered[me] = total
    for i, (g, who, k) in enumerate(group):
        started.append(send(gathered.at[me], gathered.at[me], as_.at[i], ar.at[me], who))
    for i, (g, who, k) in enumerate(group):
        arrive(gathered.at[g], as_.at[i], ar.at[g], who)

    for p in range(8):
        out_out[8 * p : 8 * p + 8] = lanes(gathered[p, 0:8], gathered[p, 8:16])
    below = [lanes(gathered[2 * t, 16:24], gathered[2 * t + 1, 16:24]) for t in range(3)]
    in_out[0:16] = rows(*below[0:2])
    in_out[16:20] = below[2][0:4]
    bias_out[...] = below[2][4:5]
    for copy in started:
        copy.wait_send()


def per_device(protocols, w_in, b_in, w_out, solved, probes, window_blocks):
    anywhere = pl.BlockSpec(memory_space=pl.ANY)
    vmem = pl.BlockSpec(memory_space=pltpu.VMEM)
    dma = pltpu.SemaphoreType.DMA
    col_grad, grad_in, grad_bias, grad_out = pl.pallas_call(
        kernel,
        out_shape=(
            jax.ShapeDtypeStruct((64, 128), F32),
            jax.ShapeDtypeStruct((20, 256), F32),
            jax.ShapeDtypeStruct((1, 256), F32),
            jax.ShapeDtypeStruct((64, 256), F32),
        ),
        in_specs=[anywhere] * 6 + [pl.BlockSpec(memory_space=pltpu.SMEM)],
        out_specs=(vmem, vmem, vmem, vmem),
        scratch_shapes=[
            pltpu.VMEM((8, 56, 128), F32),
            pltpu.VMEM((20, 256), F32),
            pltpu.VMEM((1, 256), F32),
            pltpu.VMEM((64, 256), F32),
            pltpu.VMEM((32, 128), F32),
            pltpu.VMEM((4, 16, 128), F32),
            pltpu.VMEM((4, 16, 128), F32),
            pltpu.VMEM((8, 16, 128), F32),
            pltpu.VMEM((8, 16, 128), F32),
            pltpu.VMEM((4, 256, 256), F32),
            pltpu.VMEM((4, 256, 256), BF16),
            pltpu.VMEM((4, 256, 256), BF16),
            pltpu.VMEM((4, 64, 256), F32),
            pltpu.VMEM((4, 144, 256), BF16),
            pltpu.VMEM((4, 384, 256), BF16),
            pltpu.VMEM((4, 128, 256), BF16),
            pltpu.VMEM((8, 64, 128), F32),
            pltpu.VMEM((8, 64, 128), F32),
            pltpu.VMEM((8, 24, 128), F32),
            pltpu.VMEM((8, 24, 128), F32),
            pltpu.VMEM((8, 24, 128), F32),
            pltpu.VMEM((8, 24, 128), F32),
            pltpu.VMEM((8, 24, 128), F32),
            dma((6,)),
            dma((3,)), dma((4,)),
            dma((7,)), dma((8,)),
            dma((7,)), dma((8,)),
            dma((7,)), dma((8,)),
            dma((7,)), dma((8,)),
            dma((7,)), dma((8,)),
            dma((7,)), dma((8,)),
            dma((7,)), dma((8,)),
            dma((7,)), dma((8,)),
        ],
        compiler_params=pltpu.CompilerParams(collective_id=0, has_side_effects=True),
    )(protocols, w_in, b_in.reshape(1, 256), w_out.T, solved, probes, window_blocks)
    return col_grad, grad_in, grad_bias.reshape(256), grad_out.T


def solution(mesh):
    split = P(None, ("row", "col"))
    return jax.shard_map(
        per_device,
        mesh=mesh,
        in_specs=(split, P(), P(), P(), split, split, P()),
        out_specs=(split, P(), P(), P()),
        check_vma=False,
    )
```

```python
import functools

import jax
import jax.numpy as jnp
from jax import lax
from jax.experimental import pallas as pl
from jax.experimental.pallas import tpu as pltpu
from jax.sharding import PartitionSpec as P

F32 = jnp.float32
BF16 = jnp.bfloat16
MESH = pl.DeviceIdType.MESH
RING = (4, 3, 5, 2, 6, 1, 7)


def parts2(value):
    high = value.astype(BF16).astype(F32)
    return high, value - high


def parts3(value):
    high = value.astype(BF16).astype(F32)
    rest = value - high
    middle = rest.astype(BF16).astype(F32)
    return high, middle, rest - middle


def rows(*pieces):
    return jnp.concatenate(pieces, axis=0)


def lanes(*pieces):
    return jnp.concatenate(pieces, axis=1)


def low(value):
    return value.astype(BF16)


def nn(left, right):
    return lax.dot_general(left, right, (((1,), (0,)), ((), ())), preferred_element_type=F32)


def nt(left, right):
    return lax.dot_general(left, right, (((1,), (1,)), ((), ())), preferred_element_type=F32)


def first_layer(w_in, bias):
    at = lax.broadcasted_iota(jnp.int32, (24, w_in.shape[1]), 0)
    full = rows(w_in, jnp.zeros((4, w_in.shape[1]), F32))
    full = jnp.where(at == 20, bias, full)
    h, m, l = parts3(full)
    return low(rows(h, m, h, m, h, l).T)


def second_layer(w_out):
    both = rows(*parts2(w_out))
    turned = both.T
    return low(both), low(lanes(turned, turned))


def hidden_of(first, inputs):
    h, m, l = parts3(inputs)
    return jnp.tanh(nn(first, low(rows(h, h, m, m, l, h))))


def features_of(forward, hid_h, hid_l):
    four = nn(forward, hid_h) + nn(forward, hid_l)
    return four[0:64] + four[64:128]


def ones_row(width):
    at = lax.broadcasted_iota(jnp.int32, (16, width), 0)
    return jnp.where(at == 0, 1.0, 0.0)


def stack_of(feat):
    h, l = parts2(feat)
    return low(rows(h, l, ones_row(feat.shape[1])))


def weighted(acc, own):
    return acc[0:64] + acc[64:128] - own * acc[128:129]


def column_sides(feat, vec):
    h, m, l = parts3(feat)
    one = rows(h, m).T
    two = rows(h, l).T
    v_h, v_l = parts2(vec)
    half = 0.5 * jnp.sum(feat * feat, axis=0, keepdims=True)
    half = jnp.broadcast_to(half, (128, feat.shape[1])).T
    return low(lanes(one, one, two)), low(rows(v_h, v_l, v_h, v_l).T), half


def cross_right(feat):
    h, m, l = parts3(feat)
    return low(rows(h, h, m, m, l, h))


def vec_right(vec):
    h, l = parts2(vec)
    return low(rows(h, h, l, l))


def pack(block):
    spot = lax.broadcasted_iota(jnp.int32, (16, 128), 1) // 32
    out = []
    for q in range(4):
        piece = jnp.zeros((16, 128), F32)
        for g in range(4):
            slab = block[16 * g : 16 * g + 16]
            turned = slab if g == q else pltpu.roll(slab, (32 * (g - q)) % 128, 1)
            piece = jnp.where(spot == g, turned, piece)
        out.append(piece)
    return out


def unpack(pieces):
    spot = lax.broadcasted_iota(jnp.int32, (16, 128), 1) // 32
    tiles = []
    for t in range(2):
        slabs = []
        for g in range(4):
            slab = jnp.zeros((16, 128), F32)
            for s in range(4):
                piece = pieces[4 * t + s]
                turned = piece if s == g else pltpu.roll(piece, (32 * (s - g)) % 128, 1)
                slab = jnp.where(spot == s, turned, slab)
            slabs.append(slab)
        tiles.append(rows(*slabs))
    return lanes(*tiles)


def kernel(
    protocols, w_in, b_in, w_out, solved, probes, blocks,
    col_out, in_out, bias_out, out_out,
    owners, cols, win_b, bias_b, wout_b, sol, packed, quarter, ybuf, zbuf,
    slope_b, hid_hi, hid_lo, feat_b, stack_b, cross_b, vec_b, half_b,
    colp, colr, grads, grads_x, grads_z, grads_y, grads_g,
    load_sem, known, quarter_sem, cols_sem, y_sem, z_sem, colr_sem,
    sums_x_sem, sums_z_sem, sums_y_sem, sums_g_sem,
):
    row = lax.axis_index("row")
    col = lax.axis_index("col")
    x_lo, z = row // 8, row % 8
    y, x_hi, core = col // 4, (col // 2) % 2, col % 2
    me = x_hi * 4 + x_lo * 2 + core
    mine = x_hi * 2 + core

    def device(a, b, c, d, e):
        return (b * 8 + d, c * 4 + a * 2 + e)

    def flip(value, bit):
        return 1 - value if bit else value

    loads = [
        pltpu.make_async_copy(protocols, cols.at[me, pl.ds(0, 20)], load_sem.at[0]),
        pltpu.make_async_copy(solved, sol, load_sem.at[1]),
        pltpu.make_async_copy(blocks, owners, load_sem.at[2]),
        pltpu.make_async_copy(probes, cols.at[me, pl.ds(24, 32)], load_sem.at[3]),
        pltpu.make_async_copy(w_in, win_b, load_sem.at[4]),
        pltpu.make_async_copy(b_in, bias_b, load_sem.at[5]),
        pltpu.make_async_copy(w_out, wout_b, load_sem.at[6]),
    ]
    for load in loads:
        load.start()

    group = []
    for k in (6, 7, 4, 5, 2, 3, 1):
        a, b, e = flip(x_hi, k & 4), flip(x_lo, k & 2), flip(core, k & 1)
        group.append((a * 4 + b * 2 + e, device(a, b, y, z, e), None if k & 2 else a * 2 + e))
    fours = [(q, who) for g, who, q in group if q is not None]
    group = [(g, who) for g, who, q in group]
    along_y = [((y + k) % 8, device(x_hi, x_lo, (y + k) % 8, z, core)) for k in RING]
    along_z = [((z + k) % 8, device(x_hi, x_lo, y, (z + k) % 8, core)) for k in RING]

    def at_distance(k):
        ends = [RING.index(k), RING.index(8 - k)]
        return [along_y[i][1] for i in ends] + [along_z[i][1] for i in ends]

    def greet(sem, devices):
        for who in devices:
            pl.semaphore_signal(sem, inc=1, device_id=who, device_id_type=MESH)

    barrier = pltpu.get_barrier_semaphore()
    greet(barrier, [who for g, who in group] + at_distance(1))

    finish = []

    def send(pairs, buffer, sems, here):
        for source, who in pairs:
            pltpu.make_async_remote_copy(
                src_ref=source, dst_ref=buffer.at[here], send_sem=sems.at[0], recv_sem=sems.at[1],
                device_id=who, device_id_type=MESH,
            ).start()
        count = len(pairs)
        some = buffer.at[pl.ds(0, count)]
        every = pltpu.make_async_remote_copy(
            src_ref=some, dst_ref=some, send_sem=sems.at[0], recv_sem=sems.at[1],
            device_id=pairs[0][1], device_id_type=MESH,
        )
        finish.append(every)
        return every.wait_recv

    def spread(buffer, sems, here, partners):
        return send([(buffer.at[here], who) for s, who in partners], buffer, sems, here)

    def scatter(pieces, buffer, sems, here, partners):
        return send([(pieces.at[s], who) for s, who in partners], buffer, sems, here)

    def summed(buffer, count=8):
        total = buffer[0]
        for s in range(1, count):
            total = total + buffer[s]
        return total

    at = lax.broadcasted_iota(jnp.int32, (4, 128), 0)
    cols[me, 20:24] = jnp.where(at == 0, 1.0, 0.0)
    for load in loads[0:3]:
        load.wait()

    owner = (owners[row] == col).astype(jnp.int32).astype(F32)
    block = rows(cols[me, 0:24], sol[...], jnp.zeros((8, 128), F32)) * owner
    for q, piece in enumerate(pack(block)):
        packed[q] = piece

    pl.semaphore_wait(barrier, 11)
    greet(known.at[0], at_distance(1))

    quarters_in = scatter(packed, quarter, quarter_sem, mine, fours)

    quarter[mine] = packed[mine]
    for load in loads[3:]:
        load.wait()
    first = first_layer(win_b[...], bias_b[...])
    forward, back = second_layer(wout_b[...])
    pl.semaphore_wait(known.at[0], 4)
    greet(known.at[1], at_distance(2))

    quarters_in()
    ybuf[y] = summed(quarter, 4)
    pl.semaphore_wait(known.at[1], 4)
    y_in = spread(ybuf, y_sem, y, along_y)
    cols_in = spread(cols, cols_sem, me, group)

    def columns(chunk):
        both = lanes(cols[2 * chunk], cols[2 * chunk + 1])
        inputs, vec = both[0:24], both[24:56]
        hidden = hidden_of(first, inputs)
        h, l = parts2(hidden)
        h, l = low(h), low(l)
        feat = features_of(forward, h, l)
        slope_b[chunk] = 1.0 - hidden * hidden
        hid_hi[chunk] = h
        hid_lo[chunk] = l
        feat_b[chunk] = feat
        stack_b[chunk] = stack_of(feat)
        cross_b[chunk], vec_b[chunk], half_b[chunk] = column_sides(feat, vec)

    y_in()
    zbuf[z] = summed(ybuf)
    z_in = spread(zbuf, z_sem, z, along_z)

    cols_in()
    for chunk in range(4):
        columns(chunk)

    z_in()

    window = unpack([zbuf[s] for s in range(8)])
    win_in = window[0:24]
    win_hidden = hidden_of(first, win_in)
    win_h, win_l = parts2(win_hidden)
    win_h, win_l = low(win_h), low(win_l)
    win_feat = features_of(forward, win_h, win_l)
    win_cross, win_vec = cross_right(win_feat), vec_right(window[24:56])
    win_half = 0.5 * jnp.sum(win_feat * win_feat, axis=0, keepdims=True)
    win_stack = stack_of(win_feat)

    weights = []
    for c in range(4):
        half = lanes(half_b[c], half_b[c])
        kern = jnp.exp(nn(cross_b[c], win_cross) - half - win_half)
        w_h, w_l = parts2(kern * nn(vec_b[c], win_vec))
        weights.append((low(w_h), low(w_l)))
    win_h_acc = win_l_acc = jnp.zeros((144, 256), F32)
    totals = []
    for c, (w_h, w_l) in enumerate(weights):
        part = weighted(nt(win_stack, w_h) + nt(win_stack, w_l), feat_b[c])
        win_h_acc = win_h_acc + nn(stack_b[c], w_h)
        win_l_acc = win_l_acc + nn(stack_b[c], w_l)
        colp[2 * c] = part[:, 0:128]
        colp[2 * c + 1] = part[:, 128:256]
        totals.append(part)
    totals.append(weighted(win_h_acc + win_l_acc, win_feat))

    above_h = above_l = jnp.zeros((128, 256), F32)
    below_h = below_l = jnp.zeros((48, 256), F32)
    slopes = []
    for c, part in enumerate(totals):
        part_h, part_l = parts2(part)
        both = low(rows(part_h, part_l))
        last = c == 4
        slope = 1.0 - win_hidden * win_hidden if last else slope_b[c]
        four = rows(both[0:64], both[0:64], both[64:128], both[64:128])
        slopes.append(parts2(nn(back, four) * slope))
        above_h = above_h + nt(both, win_h if last else hid_hi[c])
        above_l = above_l + nt(both, win_l if last else hid_lo[c])
    for c, (pre_h, pre_l) in enumerate(slopes):
        inputs = win_in if c == 4 else lanes(cols[2 * c, 0:24], cols[2 * c + 1, 0:24])
        left = low(rows(*parts2(inputs)))
        below_h = below_h + nt(left, low(pre_h))
        below_l = below_l + nt(left, low(pre_l))
    above, below = above_h + above_l, below_h + below_l
    above = above[0:64] + above[64:128]
    below = below[0:24] + below[24:48]
    for p in range(8):
        grads[p, 0:8] = above[8 * p : 8 * p + 8, 0:128]
        grads[p, 8:16] = above[8 * p : 8 * p + 8, 128:256]
        if p < 6:
            t, s = p // 2, p % 2
            grads[p, 16:24] = below[8 * t : 8 * t + 8, 128 * s : 128 * s + 128]
        else:
            grads[p, 16:24] = jnp.zeros((8, 128), F32)

    x_in = scatter(grads, grads_x, sums_x_sem, me, group)
    grads_x[me] = grads[me]
    x_in()
    grads_z[z] = summed(grads_x)

    z_in = spread(grads_z, sums_z_sem, z, along_z)
    colr_in = scatter(colp, colr, colr_sem, me, group)
    colr[me] = colp[me]
    z_in()
    grads_y[y] = summed(grads_z)

    y_in = spread(grads_y, sums_y_sem, y, along_y)
    colr_in()
    col_out[...] = summed(colr)
    y_in()
    grads_g[me] = summed(grads_y)

    g_in = spread(grads_g, sums_g_sem, me, group)
    for every in finish[:-1]:
        every.wait_send()
    g_in()

    for p in range(8):
        out_out[8 * p : 8 * p + 8] = lanes(grads_g[p, 0:8], grads_g[p, 8:16])
    below = [lanes(grads_g[2 * t, 16:24], grads_g[2 * t + 1, 16:24]) for t in range(3)]
    in_out[0:16] = rows(*below[0:2])
    in_out[16:20] = below[2][0:4]
    bias_out[...] = below[2][4:5]
    finish[-1].wait_send()


SHAPES = ((64, 128), (20, 256), (1, 256), (64, 256))


def write_out(a, b, c, d, a_out, b_out, c_out, d_out, sems):
    pairs = ((a, a_out), (b, b_out), (c, c_out), (d, d_out))
    copies = [pltpu.make_async_copy(s, t, sems.at[i]) for i, (s, t) in enumerate(pairs)]
    for copy in copies:
        copy.start()
    for copy in copies:
        copy.wait()


def per_device(protocols, w_in, b_in, w_out, solved, probes, window_blocks):
    anywhere = pl.BlockSpec(memory_space=pl.ANY)
    vmem = pl.BlockSpec(memory_space=pltpu.VMEM)
    dma = pltpu.SemaphoreType.DMA
    results = pl.pallas_call(
        kernel,
        out_shape=tuple(pltpu.VMEM(shape, F32) for shape in SHAPES),
        in_specs=[anywhere] * 7,
        out_specs=(vmem, vmem, vmem, vmem),
        scratch_shapes=[
            pltpu.SMEM((16,), jnp.int32),
            pltpu.VMEM((8, 56, 128), F32),
            pltpu.VMEM((20, 256), F32),
            pltpu.VMEM((1, 256), F32),
            pltpu.VMEM((64, 256), F32),
            pltpu.VMEM((32, 128), F32),
            pltpu.VMEM((4, 16, 128), F32),
            pltpu.VMEM((4, 16, 128), F32),
            pltpu.VMEM((8, 16, 128), F32),
            pltpu.VMEM((8, 16, 128), F32),
            pltpu.VMEM((4, 256, 256), F32),
            pltpu.VMEM((4, 256, 256), BF16),
            pltpu.VMEM((4, 256, 256), BF16),
            pltpu.VMEM((4, 64, 256), F32),
            pltpu.VMEM((4, 144, 256), BF16),
            pltpu.VMEM((4, 256, 384), BF16),
            pltpu.VMEM((4, 256, 128), BF16),
            pltpu.VMEM((4, 256, 128), F32),
            pltpu.VMEM((8, 64, 128), F32),
            pltpu.VMEM((8, 64, 128), F32),
            *[pltpu.VMEM((8, 24, 128), F32)] * 5,
            dma((7,)),
            pltpu.SemaphoreType.REGULAR((2,)),
            *[dma((2,))] * 9,
        ],
        compiler_params=pltpu.CompilerParams(collective_id=0, has_side_effects=True),
    )(protocols, w_in, b_in.reshape(1, 256), w_out.T, solved, probes, window_blocks)
    col_grad, grad_in, grad_bias, grad_out = pl.pallas_call(
        write_out,
        out_shape=tuple(jax.ShapeDtypeStruct(shape, F32) for shape in SHAPES),
        in_specs=[vmem] * 4,
        out_specs=(anywhere,) * 4,
        scratch_shapes=[dma((4,))],
    )(*[pltpu.with_memory_space_constraint(v, pltpu.VMEM) for v in results])
    return col_grad, grad_in, grad_bias.reshape(256), grad_out.T


def solution(mesh):
    split = P(None, ("row", "col"))
    return jax.shard_map(
        per_device,
        mesh=mesh,
        in_specs=(split, P(), P(), P(), split, split, P()),
        out_specs=(split, P(), P(), P()),
        check_vma=False,
    )
```
